32 devices in a mesh: replica: 2 (over y), shard: 2 (over x), tensor: 8 (over z, core).
Axes of the slice: x: 2, y: 2, z: 4, core: 2. Of those that a mesh axis runs over, the one named last changes fastest.
Arguments:
- layer_input: bfloat16 [32768, 1024], P(('replica', 'shard', 'tensor')), may hold values from -6 to 6
- segment_ids: int32 [32, 1024], P(('replica', 'shard')), may hold values from 0 to 3, as said below
- qkv_weight: bfloat16 [3, 1024, 1024], P(None, 'shard', 'tensor'), may hold values from -0.1875 to 0.1875
- qkv_bias: float32 [2, 1024], P(None, 'tensor'), may hold values from -1.2 to 1.2
- out_weight: bfloat16 [1024, 1024], P('tensor', 'shard'), may hold values from -1.5 to 1.5
- out_bias: float32 [1024], replicated, may hold values from -3 to 3
- norm1_gain: float32 [1024], replicated, may hold values from 0.5 to 1.5
- norm1_bias: float32 [1024], replicated, may hold values from -3 to 3
- up_weight: bfloat16 [1024, 4096], P('shard', 'tensor'), may hold values from -0.1875 to 0.1875
- up_bias: float32 [4096], P('tensor'), may hold values from -3 to 3
- down_weight: bfloat16 [4096, 1024], P('tensor', 'shard'), may hold values from -0.09375 to 0.09375
- down_bias: float32 [1024], replicated, may hold values from -3 to 3
- norm2_gain: float32 [1024], replicated, may hold values from 0.5 to 1.5
- norm2_bias: float32 [1024], replicated, may hold values from -3 to 3
- output_grad: bfloat16 [32768, 1024], P(('replica', 'shard', 'tensor')), may hold values from -6 to 6
Outputs:
- activations: bfloat16 [32768, 1024], P(('replica', 'shard', 'tensor'))
- input_grad: float32 [32768, 1024], P(('replica', 'shard', 'tensor'))
- qkv_weight_grad: float32 [3, 1024, 1024], P(None, 'shard', 'tensor')
- qkv_bias_grad: float32 [2, 1024], P(None, 'tensor')
- out_weight_grad: float32 [1024, 1024], P('tensor', 'shard')
- out_bias_grad: float32 [1024], replicated
- norm1_gain_grad: float32 [1024], replicated
- norm1_bias_grad: float32 [1024], replicated
- up_weight_grad: float32 [1024, 4096], P('shard', 'tensor')
- up_bias_grad: float32 [4096], P('tensor')
- down_weight_grad: float32 [4096, 1024], P('tensor', 'shard')
- down_bias_grad: float32 [1024], replicated
- norm2_gain_grad: float32 [1024], replicated
- norm2_bias_grad: float32 [1024], replicated
The draws below stay inside these ranges and needn't reach their ends.
Inputs may be any that keep to these rules, and one draw needn't show every extreme that they name: `segment_ids`: within each sequence the ids never fall and every id from 0 to 3 occurs; each document holds 128 to 512 tokens, and one in each sequence holds exactly 512.
All inputs are finite; a program needn't handle non-finite values.
Results may differ from the reference program's by a relative error of at most 0.02.
Values may be sent and summed in bfloat16 or wider, within the bound.
No kernel may reach another device: no remote copies, remote signals or barrier semaphores. Data moves between devices by JAX's collectives and lax.ppermute only.
A program may use at most 256 MiB of HBM per device.

```python
import math
import jax
import jax.numpy as jnp
from jax import lax

D = 1024
HEADS = 16
HEAD_DIM = 64
FF = 4096
LEN = 1024
DOCS = 4
SEQS = 32
TOKENS = 32768


def draw_segment_ids(key, part):
    key_big = jax.random.fold_in(key, 11)
    key_cut = jax.random.fold_in(key, 23)
    least = LEN // 8
    spare = LEN // 2 - (DOCS - 1) * least
    big_slot = jax.random.randint(key_big, (SEQS, 1), 0, DOCS)
    cuts = jnp.sort(jax.random.randint(key_cut, (SEQS, DOCS - 2), 0, spare + 1), axis=1)
    bounds = jnp.concatenate([jnp.zeros((SEQS, 1), jnp.int32), cuts.astype(jnp.int32), jnp.full((SEQS, 1), spare, jnp.int32)], axis=1)
    small = bounds[:, 1:] - bounds[:, :-1] + least
    slots = jnp.arange(DOCS, dtype=jnp.int32)[None, :]
    source = jnp.clip(jnp.where(slots > big_slot, slots - 1, slots), 0, DOCS - 2)
    picked = jnp.take_along_axis(small, source, axis=1)
    lengths = jnp.where(slots == big_slot, LEN // 2, picked).astype(jnp.int32)
    ends = jnp.cumsum(lengths, axis=1)
    places = jnp.arange(LEN, dtype=jnp.int32)[None, :, None]
    return jnp.sum((places >= ends[:, None, :DOCS - 1]).astype(jnp.int32), axis=-1).astype(jnp.int32)


def level_of(key, shape, cuts, smallest, largest):
    def one(axis_at, parts):
        heights = jax.random.uniform(jax.random.fold_in(jax.random.fold_in(key, 6), axis_at), (parts,), jnp.float32, smallest / len(cuts), largest / len(cuts))
        return jnp.repeat(jnp.exp(heights), shape[axis_at] // parts).reshape((-1,) + (1,) * (len(shape) - axis_at - 1))

    gain = one(*cuts[0])
    for cut in cuts[1:]:
        gain = gain * one(*cut)
    return gain


def normal_values(stream_key, shape, scale, reach, pieces=(), kind=jnp.bfloat16):
    array = jax.random.normal(stream_key, shape, jnp.float32) * scale
    if len(pieces) > 0:
        array = level_of(stream_key, shape, pieces, -0.22, 0.18) * array
    return jnp.clip(array, min=-reach, max=reach).astype(kind)


def setup_inputs(seed: int = 0) -> dict:
    keys = jax.random.split(jax.random.key(seed), 16)
    return {
        "layer_input": normal_values(keys[0], (TOKENS, D), 1.0, 6.0, ((0, 32),)),
        "segment_ids": draw_segment_ids(jax.random.fold_in(keys[15], 71), 0),
        "qkv_weight": normal_values(keys[2], (3, D, D), D ** -0.5, 0.1875, ((1, 2), (2, 8))),
        "qkv_bias": normal_values(keys[3], (2, D), 0.2, 1.2, ((1, 8),), jnp.float32),
        "out_weight": normal_values(keys[4], (D, D), (max(1, D * 16 // LEN)) ** -0.5, 1.5, ((0, 8), (1, 2))),
        "out_bias": normal_values(keys[5], (D,), 0.5, 3.0, (), jnp.float32),
        "norm1_gain": jnp.clip(1.0 + 0.1 * jax.random.normal(keys[6], (D,), jnp.float32), 0.5, 1.5),
        "norm1_bias": normal_values(keys[7], (D,), 0.5, 3.0, (), jnp.float32),
        "up_weight": normal_values(keys[8], (D, FF), D ** -0.5, 0.1875, ((0, 2), (1, 8))),
        "up_bias": normal_values(keys[9], (FF,), 0.5, 3.0, ((0, 8),), jnp.float32),
        "down_weight": normal_values(keys[10], (FF, D), FF ** -0.5, 0.09375, ((0, 8), (1, 2))),
        "down_bias": normal_values(keys[11], (D,), 0.5, 3.0, (), jnp.float32),
        "norm2_gain": jnp.clip(1.0 + 0.1 * jax.random.normal(keys[12], (D,), jnp.float32), 0.5, 1.5),
        "norm2_bias": normal_values(keys[13], (D,), 0.5, 3.0, (), jnp.float32),
        "output_grad": normal_values(keys[14], (TOKENS, D), 1.0, 6.0, ((0, 32),)),
    }


@jax.custom_vjp
def low(v):
    return lax.optimization_barrier(v.astype(jnp.bfloat16)).astype(jnp.float32)

@jax.custom_vjp
def low_back(v):
    return v

def low_keep(v):
    return (low(v), None)

def low_pass(kept, grad):
    return (grad,)

def back_keep(v):
    return (v, None)

def back_low(kept, grad):
    return (low(grad),)
low.defvjp(low_keep, low_pass)
low_back.defvjp(back_keep, back_low)
EPSILON = 1e-05
NEG_FILL = -1e+30
PRECISE = lax.Precision.HIGHEST

def matmul(left_side, right_side):
    return jnp.dot(left_side, right_side, precision=PRECISE, preferred_element_type=jnp.float32)

def normalize(residual, gain_vec, shift_vec):
    center = residual - lax.optimization_barrier(jnp.mean(residual, axis=-1, keepdims=True))
    spread = lax.rsqrt(lax.optimization_barrier(jnp.mean(center * center, axis=-1, keepdims=True)) + EPSILON)
    return center * spread * gain_vec + shift_vec

def attention(queries, key_rows, value_rows, segments):
    scores = low_back(jnp.einsum('qhd,khd->hqk', queries, key_rows, precision=PRECISE) * HEAD_DIM ** (-0.5))
    same_doc = segments[:, None] == segments[None, :]
    masked = jnp.where(same_doc[None], scores, NEG_FILL)
    row_max = lax.optimization_barrier(jnp.max(masked, axis=-1, keepdims=True))
    raw_weights = jnp.exp(masked - row_max)
    attn_probs = raw_weights / lax.optimization_barrier(jnp.sum(raw_weights, axis=-1, keepdims=True))
    mixed_heads = jnp.einsum('hqk,khd->qhd', low(attn_probs), value_rows, precision=PRECISE)
    return low(low_back(mixed_heads)).reshape(LEN, HEADS * HEAD_DIM)

def attend_item(block_item):
    return attention(block_item[0], block_item[1], block_item[2], block_item[3])

def split_heads(rows_array, seq_count):
    return rows_array.reshape(seq_count, LEN, HEADS, HEAD_DIM)

def layer(tokens, segments, params):
    qkv_w, qkv_b, out_w, out_b, gain_one, shift_one, up_w, up_b, down_w, down_b, gain_two, shift_two = params
    seq_count = tokens.shape[0] // LEN
    queries = low(low_back(matmul(tokens, qkv_w[0])) + qkv_b[0])
    key_rows = low(low_back(matmul(tokens, qkv_w[1])))
    value_rows = low(low_back(matmul(tokens, qkv_w[2])) + qkv_b[1])
    mixed = lax.map(jax.checkpoint(attend_item), (split_heads(queries, seq_count), split_heads(key_rows, seq_count), split_heads(value_rows, seq_count), segments))
    mixed_rows = mixed.reshape(seq_count * LEN, D)
    residual_one = tokens + low_back(matmul(mixed_rows, out_w)) + out_b
    hidden_one = normalize(residual_one, gain_one, shift_one)
    pre_act = low_back(matmul(low(hidden_one), up_w)) + up_b
    activ = low(jax.nn.gelu(pre_act, approximate=False))
    residual_two = hidden_one + low_back(matmul(activ, down_w)) + down_b
    return normalize(residual_two, gain_two, shift_two)

def reference(layer_input, segment_ids, qkv_weight, qkv_bias, out_weight, out_bias, norm1_gain, norm1_bias, up_weight, up_bias, down_weight, down_bias, norm2_gain, norm2_bias, output_grad):
    params = tuple((arr.astype(jnp.float32) for arr in (qkv_weight, qkv_bias, out_weight, out_bias, norm1_gain, norm1_bias, up_weight, up_bias, down_weight, down_bias, norm2_gain, norm2_bias)))
    group_size = math.gcd(SEQS, 4)
    block_count = SEQS // group_size
    tok_blocks = layer_input.astype(jnp.float32).reshape(block_count, group_size * LEN, D)
    grad_blocks = output_grad.astype(jnp.float32).reshape(block_count, group_size * LEN, D)
    seg_blocks = segment_ids.reshape(block_count, group_size, LEN)

    def step(running, block_item):
        tok_block, grad_block, seg_block = block_item

        def forward(tok_arg, param_arg):
            return layer(tok_arg, seg_block, param_arg)
        result, pullback = jax.vjp(forward, tok_block, params)
        tok_grad, param_grad = pullback(grad_block)
        running = jax.tree.map(jnp.add, running, param_grad)
        return (running, (result, tok_grad))
    initial = jax.tree.map(jnp.zeros_like, params)
    totals, (results, tok_grads) = lax.scan(step, initial, (tok_blocks, grad_blocks, seg_blocks))
    return (results.reshape(TOKENS, D).astype(jnp.bfloat16), tok_grads.reshape(TOKENS, D), totals[0], totals[1], totals[2], totals[3], totals[4], totals[5], totals[6], totals[7], totals[8], totals[9], totals[10], totals[11])
```

```python
import math

import jax
import jax.numpy as jnp
from jax import lax
from jax.sharding import PartitionSpec as P

HEAD_DIM = 64
LEN = 1024

EPSILON = 1e-05
NEG_FILL = -1e30
CONTRACT_ROWS = (((0,), (0,)), ((), ()))
CONTRACT_COLS = (((1,), (1,)), ((), ()))
OWNERS = ("shard", "tensor")
EVERYONE = ("replica", "shard", "tensor")


def gather_blocks(weight):
    blocks = lax.all_gather(weight, OWNERS, axis=0, tiled=False)
    return blocks.reshape((lax.axis_size("shard"), lax.axis_size("tensor")) + weight.shape)


def gather_qkv(weight):
    blocks = gather_blocks(weight)
    return blocks.transpose(2, 0, 3, 1, 4).reshape(3, -1, blocks.shape[1] * blocks.shape[4])


def gather_row_col(weight):
    blocks = gather_blocks(weight)
    return blocks.transpose(0, 2, 1, 3).reshape(-1, blocks.shape[1] * blocks.shape[3])


def gather_col_row(weight):
    blocks = gather_blocks(weight)
    return blocks.transpose(1, 2, 0, 3).reshape(-1, blocks.shape[0] * blocks.shape[3])


def scatter_blocks(blocks):
    flat = blocks.reshape((-1,) + blocks.shape[2:])
    owned = lax.psum_scatter(flat, OWNERS, scatter_dimension=0, tiled=False)
    return lax.psum(owned, "replica").astype(jnp.float32)


def scatter_qkv(grad):
    shards, tensors = lax.axis_size("shard"), lax.axis_size("tensor")
    three, rows, cols = grad.shape
    blocks = grad.reshape(three, shards, rows // shards, tensors, cols // tensors)
    return scatter_blocks(blocks.transpose(1, 3, 0, 2, 4))


def scatter_row_col(grad):
    shards, tensors = lax.axis_size("shard"), lax.axis_size("tensor")
    rows, cols = grad.shape
    blocks = grad.reshape(shards, rows // shards, tensors, cols // tensors)
    return scatter_blocks(blocks.transpose(0, 2, 1, 3))


def scatter_col_row(grad):
    shards, tensors = lax.axis_size("shard"), lax.axis_size("tensor")
    rows, cols = grad.shape
    blocks = grad.reshape(tensors, rows // tensors, shards, cols // shards)
    return scatter_blocks(blocks.transpose(2, 0, 1, 3))


def normalize(residual, gain_vec, shift_vec):
    center = residual - jnp.mean(residual, axis=-1, keepdims=True)
    spread = lax.rsqrt(jnp.mean(center * center, axis=-1, keepdims=True) + EPSILON)
    normed = center * spread
    return (normed * gain_vec + shift_vec, normed, spread)


def norm_back(incoming, normed, spread, gain_vec):
    scaled = incoming * gain_vec
    back_grad = spread * (
        scaled
        - jnp.mean(scaled, axis=-1, keepdims=True)
        - normed * jnp.mean(scaled * normed, axis=-1, keepdims=True)
    )
    return (back_grad, jnp.sum(incoming * normed, axis=0), jnp.sum(incoming, axis=0))


def masked_scores(queries, key_rows, same_doc):
    scores = jnp.einsum(
        "qhd,khd->hqk", queries, key_rows, preferred_element_type=jnp.float32
    ) * HEAD_DIM ** (-0.5)
    return jnp.where(same_doc[None], scores, NEG_FILL)


def attend(queries, key_rows, value_rows, same_doc):
    scores = masked_scores(queries, key_rows, same_doc)
    row_max = jnp.max(scores, axis=-1, keepdims=True)
    raw_weights = jnp.exp(scores - row_max)
    row_total = jnp.sum(raw_weights, axis=-1, keepdims=True)
    attn_probs = raw_weights / row_total
    log_total = row_max + jnp.log(row_total)
    mixed_heads = jnp.einsum(
        "hqk,khd->qhd",
        attn_probs.astype(jnp.bfloat16),
        value_rows,
        preferred_element_type=jnp.float32,
    )
    return (mixed_heads.astype(jnp.bfloat16), log_total)


def attend_back(queries, key_rows, value_rows, same_doc, log_total, mixed_grad):
    scores = masked_scores(queries, key_rows, same_doc)
    attn_probs = jnp.exp(scores - log_total)
    prob_grad = jnp.einsum(
        "qhd,khd->hqk", mixed_grad, value_rows, preferred_element_type=jnp.float32
    )
    value_grad = jnp.einsum(
        "hqk,qhd->khd",
        attn_probs.astype(jnp.bfloat16),
        mixed_grad,
        preferred_element_type=jnp.float32,
    )
    inner_sum = jnp.sum(attn_probs * prob_grad, axis=-1, keepdims=True)
    score_low = (attn_probs * (prob_grad - inner_sum)).astype(jnp.bfloat16)
    query_grad = jnp.einsum(
        "hqk,khd->qhd", score_low, key_rows, preferred_element_type=jnp.float32
    ) * HEAD_DIM ** (-0.5)
    key_grad = jnp.einsum(
        "hqk,qhd->khd", score_low, queries, preferred_element_type=jnp.float32
    ) * HEAD_DIM ** (-0.5)
    return (query_grad, key_grad, value_grad)


def body(
    layer_input,
    segment_ids,
    qkv_weight,
    qkv_bias,
    out_weight,
    out_bias,
    norm1_gain,
    norm1_bias,
    up_weight,
    up_bias,
    down_weight,
    down_bias,
    norm2_gain,
    norm2_bias,
    output_grad,
):
    rows, width = layer_input.shape
    tensor_index = lax.axis_index("tensor")
    tensor_count = lax.axis_size("tensor")
    sharers = max(1, LEN // rows)
    seqs_here = max(1, rows // LEN)
    query_rows = min(rows, LEN)
    sharing = [list(range(i, i + sharers)) for i in range(0, tensor_count, sharers)]

    w_qkv = gather_qkv(qkv_weight)
    bias_qkv = lax.all_gather(qkv_bias, "tensor", axis=1, tiled=True)
    bias_up = lax.all_gather(up_bias, "tensor", axis=0, tiled=True)
    w_out = gather_col_row(out_weight)
    w_up = gather_row_col(up_weight)
    w_down = gather_col_row(down_weight)

    first_seq = tensor_index * rows // LEN
    key_segments = lax.dynamic_slice_in_dim(segment_ids, first_seq, seqs_here, 0)
    query_start = tensor_index * rows % LEN
    query_segments = lax.dynamic_slice_in_dim(key_segments, query_start, query_rows, 1)
    same_doc = query_segments[:, :, None] == key_segments[:, None, :]

    heads = width // HEAD_DIM
    group = 2

    def by_head(rows_array, length):
        split = rows_array.reshape(seqs_here, length, heads // group, group, HEAD_DIM)
        return split.transpose(0, 2, 1, 3, 4)

    def from_heads(blocks):
        return blocks.transpose(0, 2, 1, 3, 4).reshape(-1, width)

    def whole_rows(rows_array):
        if sharers == 1:
            return rows_array
        return lax.all_gather(rows_array, "tensor", axis_index_groups=sharing, axis=0, tiled=True)

    def own_rows(rows_array):
        if sharers == 1:
            return rows_array
        return lax.psum_scatter(
            rows_array, "tensor", axis_index_groups=sharing, scatter_dimension=0, tiled=True
        )

    projected = jnp.einsum("td,jdc->jtc", layer_input, w_qkv, preferred_element_type=jnp.float32)
    queries = (projected[0] + bias_qkv[0]).astype(jnp.bfloat16)
    key_rows = whole_rows(projected[1].astype(jnp.bfloat16))
    value_rows = whole_rows((projected[2] + bias_qkv[1]).astype(jnp.bfloat16))
    queries = by_head(queries, query_rows)
    key_rows = by_head(key_rows, LEN)
    value_rows = by_head(value_rows, LEN)
    mixed, log_total = [], []
    for s in range(seqs_here):
        one_mixed, one_log = lax.map(
            lambda item: attend(*item, same_doc[s]), (queries[s], key_rows[s], value_rows[s])
        )
        mixed.append(one_mixed)
        log_total.append(one_log)
    mixed_rows = from_heads(jnp.stack(mixed))
    residual_one = (
        layer_input.astype(jnp.float32)
        + jnp.dot(mixed_rows, w_out, preferred_element_type=jnp.float32)
        + out_bias
    )
    hidden_one, normed_one, spread_one = normalize(residual_one, norm1_gain, norm1_bias)
    hidden_low = hidden_one.astype(jnp.bfloat16)
    pre_act = jnp.dot(hidden_low, w_up, preferred_element_type=jnp.float32) + bias_up
    activ = jax.nn.gelu(pre_act, approximate=False).astype(jnp.bfloat16)
    residual_two = (
        hidden_one + jnp.dot(activ, w_down, preferred_element_type=jnp.float32) + down_bias
    )
    final_out, normed_two, spread_two = normalize(residual_two, norm2_gain, norm2_bias)
    resid_two_grad, gain_two_grad, shift_two_grad = norm_back(
        output_grad.astype(jnp.float32), normed_two, spread_two, norm2_gain
    )
    down_bias_part = jnp.sum(resid_two_grad, axis=0)
    branch_grad = resid_two_grad.astype(jnp.bfloat16)
    down_grad = lax.dot_general(
        activ, branch_grad, CONTRACT_ROWS, preferred_element_type=jnp.float32
    ).astype(jnp.bfloat16)
    down_owned = scatter_col_row(down_grad)
    activ_grad = lax.dot_general(
        branch_grad, w_down, CONTRACT_COLS, preferred_element_type=jnp.float32
    )
    normal_cdf = 0.5 * (1.0 + lax.erf(pre_act * (1.0 / math.sqrt(2.0))))
    normal_pdf = jnp.exp(-0.5 * pre_act * pre_act) * (1.0 / math.sqrt(2.0 * math.pi))
    pre_grad = activ_grad * (normal_cdf + pre_act * normal_pdf)
    up_bias_part = jnp.sum(pre_grad, axis=0)
    pre_low = pre_grad.astype(jnp.bfloat16)
    up_grad = lax.dot_general(
        hidden_low, pre_low, CONTRACT_ROWS, preferred_element_type=jnp.float32
    ).astype(jnp.bfloat16)
    up_owned = scatter_row_col(up_grad)
    back_middle = lax.dot_general(pre_low, w_up, CONTRACT_COLS, preferred_element_type=jnp.float32)
    resid_one_grad, gain_one_grad, shift_one_grad = norm_back(
        resid_two_grad + back_middle, normed_one, spread_one, norm1_gain
    )
    out_bias_part = jnp.sum(resid_one_grad, axis=0)
    attn_grad = resid_one_grad.astype(jnp.bfloat16)
    out_grad = lax.dot_general(
        mixed_rows, attn_grad, CONTRACT_ROWS, preferred_element_type=jnp.float32
    ).astype(jnp.bfloat16)
    out_owned = scatter_col_row(out_grad)
    mixed_grad = lax.dot_general(
        attn_grad, w_out, CONTRACT_COLS, preferred_element_type=jnp.float32
    ).astype(jnp.bfloat16)
    mixed_grad = by_head(mixed_grad, query_rows)
    query_grad, key_grad, value_grad = [], [], []
    for s in range(seqs_here):
        grads = lax.map(
            lambda item: attend_back(item[0], item[1], item[2], same_doc[s], item[3], item[4]),
            (queries[s], key_rows[s], value_rows[s], log_total[s], mixed_grad[s]),
        )
        query_grad.append(grads[0])
        key_grad.append(grads[1])
        value_grad.append(grads[2])
    query_grad = from_heads(jnp.stack(query_grad))
    key_grad = own_rows(from_heads(jnp.stack(key_grad)))
    value_grad = own_rows(from_heads(jnp.stack(value_grad)))
    proj_low = [grad.astype(jnp.bfloat16) for grad in (query_grad, key_grad, value_grad)]
    qkv_grad = jnp.stack(
        [
            lax.dot_general(
                layer_input, grad, CONTRACT_ROWS, preferred_element_type=jnp.float32
            ).astype(jnp.bfloat16)
            for grad in proj_low
        ]
    )
    qkv_owned = scatter_qkv(qkv_grad)
    input_grad = resid_one_grad
    for j in range(3):
        input_grad = input_grad + lax.dot_general(
            proj_low[j], w_qkv[j], CONTRACT_COLS, preferred_element_type=jnp.float32
        )
    parts = (
        jnp.sum(query_grad, axis=0),
        jnp.sum(value_grad, axis=0),
        up_bias_part,
        out_bias_part,
        gain_one_grad,
        shift_one_grad,
        down_bias_part,
        gain_two_grad,
        shift_two_grad,
    )
    summed = jnp.sum(lax.all_gather(jnp.concatenate(parts), EVERYONE, axis=0, tiled=False), axis=0)
    ends = [0]
    for part in parts:
        ends.append(ends[-1] + part.shape[0])
    summed = [summed[ends[i] : ends[i + 1]] for i in range(len(parts))]
    width_here = qkv_bias.shape[1]
    hidden_here = up_bias.shape[0]
    qkv_bias_grad = lax.dynamic_slice_in_dim(
        jnp.stack(summed[:2]), tensor_index * width_here, width_here, 1
    )
    up_bias_grad = lax.dynamic_slice_in_dim(summed[2], tensor_index * hidden_here, hidden_here, 0)
    return (
        final_out.astype(jnp.bfloat16),
        input_grad,
        qkv_owned,
        qkv_bias_grad,
        out_owned,
        summed[3],
        summed[4],
        summed[5],
        up_owned,
        up_bias_grad,
        down_owned,
        summed[6],
        summed[7],
        summed[8],
    )


def solution(mesh):
    placed = (
        P(("replica", "shard", "tensor"), None),
        P(("replica", "shard"), None),
        P(None, "shard", "tensor"),
        P(None, "tensor"),
        P("tensor", "shard"),
        P(),
        P(),
        P(),
        P("shard", "tensor"),
        P("tensor"),
        P("tensor", "shard"),
        P(),
        P(),
        P(),
        P(("replica", "shard", "tensor"), None),
    )
    return jax.shard_map(
        body,
        mesh=mesh,
        in_specs=placed,
        out_specs=(
            P(("replica", "shard", "tensor"), None),
            P(("replica", "shard", "tensor"), None),
            P(None, "shard", "tensor"),
            P(None, "tensor"),
            P("tensor", "shard"),
            P(),
            P(),
            P(),
            P("shard", "tensor"),
            P("tensor"),
            P("tensor", "shard"),
            P(),
            P(),
            P(),
        ),
        check_vma=False,
    )
```

```python
import jax
import jax.numpy as jnp
from jax import lax
from jax.experimental.layout import Layout, with_layout_constraint
from jax.experimental import pallas as pl
from jax.experimental.pallas import tpu as pltpu
from jax.sharding import PartitionSpec as P


import math

HEAD_DIM = 64
LEN = 1024
BLOCK = 256
PAIR = 128
FAR = 1e15
SCALE = HEAD_DIM ** (-0.5)
EPSILON = 1e-05
OWNERS = ("shard", "tensor")
EVERYONE = ("replica", "shard", "tensor")


def lanes_of(head, rows):
    lane = lax.broadcasted_iota(jnp.int32, (rows, PAIR), 1)
    return (lane // HEAD_DIM) == head


def with_marks(rows_block, marks, head):
    return jnp.where(lanes_of(head, rows_block.shape[0]), rows_block, marks)


def only_head(rows_block, head):
    return jnp.where(lanes_of(head, rows_block.shape[0]), rows_block, jnp.zeros_like(rows_block))


def attend_kernel(bounds, q_ref, k_ref, v_ref, qmark_ref, kmark_ref, o_ref, lse_ref):
    s_id = pl.program_id(0)
    blocks = q_ref.shape[0] // BLOCK
    for qb in range(blocks):
        rows = slice(qb * BLOCK, (qb + 1) * BLOCK)
        q = q_ref[rows, :]
        qmark = qmark_ref[rows, :]
        q_aug = [with_marks(q, qmark, h) for h in range(2)]

        def step(kb, carry):
            keys = pl.ds(pl.multiple_of(kb * BLOCK, BLOCK), BLOCK)
            k = k_ref[keys, :]
            v = v_ref[keys, :]
            kmark = kmark_ref[keys, :]
            out = []
            for h in range(2):
                top, total, acc = carry[h]
                scores = lax.dot_general(q_aug[h], with_marks(k, kmark, h), (((1,), (1,)), ((), ())),
                                         preferred_element_type=jnp.float32)
                new_top = jnp.maximum(top, jnp.max(scores, axis=-1, keepdims=True))
                fade = jnp.exp(top - new_top)
                weights = jnp.exp(scores - new_top)
                total = total * fade + jnp.sum(weights, axis=-1, keepdims=True)
                acc = acc * fade + jnp.dot(weights.astype(jnp.bfloat16), v, preferred_element_type=jnp.float32)
                out.append((new_top, total, acc))
            return tuple(out)

        start = tuple((jnp.full((BLOCK, 1), -3e38, jnp.float32), jnp.zeros((BLOCK, 1), jnp.float32),
                       jnp.zeros((BLOCK, PAIR), jnp.float32)) for _ in range(2))
        done = lax.fori_loop(bounds[s_id, 0, qb], bounds[s_id, 1, qb], step, start)
        (m0, l0, a0), (m1, l1, a1) = done
        o_ref[rows, :] = jnp.where(lanes_of(0, BLOCK), a0 / l0, a1 / l1).astype(o_ref.dtype)
        lse = jnp.where(lanes_of(0, BLOCK), m0 + jnp.log(l0), m1 + jnp.log(l1))
        flat = jnp.transpose(lse)
        lse_ref[0:1, rows] = flat[0:1, :]
        lse_ref[1:2, rows] = flat[HEAD_DIM:HEAD_DIM + 1, :]


def attend_back_kernel(bounds, q_ref, k_ref, v_ref, qmark_ref, kmark_ref, lse_ref, o_ref, do_ref,
                       dq_ref, dk_ref, dv_ref, dq_acc, delta_acc):
    s_id = pl.program_id(0)
    q_blocks = q_ref.shape[0] // BLOCK
    dq_acc[...] = jnp.zeros_like(dq_acc)
    for qb in range(q_blocks):
        rows = slice(qb * BLOCK, (qb + 1) * BLOCK)
        prod = do_ref[rows, :].astype(jnp.float32) * o_ref[rows, :].astype(jnp.float32)
        flat = jnp.transpose(prod)
        delta_acc[0:1, rows] = jnp.sum(flat[:HEAD_DIM, :], axis=0, keepdims=True)
        delta_acc[1:2, rows] = jnp.sum(flat[HEAD_DIM:, :], axis=0, keepdims=True)
    for kb in range(k_ref.shape[0] // BLOCK):
        keys = slice(kb * BLOCK, (kb + 1) * BLOCK)
        k = k_ref[keys, :]
        v = v_ref[keys, :]
        kmark = kmark_ref[keys, :]
        k_aug = [with_marks(k, kmark, h) for h in range(2)]
        v_own = [only_head(v, h) for h in range(2)]

        def step(qb, carry):
            rows = pl.ds(pl.multiple_of(qb * BLOCK, BLOCK), BLOCK)
            q = q_ref[rows, :]
            do = do_ref[rows, :]
            qmark = qmark_ref[rows, :]
            out, dq_parts = [], []
            for h in range(2):
                dk, dv = carry[h]
                scores = lax.dot_general(k_aug[h], with_marks(q, qmark, h), (((1,), (1,)), ((), ())),
                                         preferred_element_type=jnp.float32)
                probs = jnp.exp(scores - lse_ref[h:h + 1, rows])
                prob_grad = lax.dot_general(v_own[h], do, (((1,), (1,)), ((), ())),
                                            preferred_element_type=jnp.float32)
                score_low = (probs * (prob_grad - delta_acc[h:h + 1, rows])).astype(jnp.bfloat16)
                dv = dv + jnp.dot(probs.astype(jnp.bfloat16), do, preferred_element_type=jnp.float32)
                dk = dk + jnp.dot(score_low, q, preferred_element_type=jnp.float32)
                dq_parts.append(lax.dot_general(score_low, k, (((0,), (0,)), ((), ())),
                                                preferred_element_type=jnp.float32))
                out.append((dk, dv))
            dq_acc[rows, :] += jnp.where(lanes_of(0, BLOCK), dq_parts[0], dq_parts[1])
            return tuple(out)

        zero = jnp.zeros((BLOCK, PAIR), jnp.float32)
        done = lax.fori_loop(bounds[s_id, 2, kb], bounds[s_id, 3, kb], step, ((zero, zero), (zero, zero)))
        dk_ref[keys, :] = jnp.where(lanes_of(0, BLOCK), done[0][0], done[1][0]).astype(dk_ref.dtype)
        dv_ref[keys, :] = jnp.where(lanes_of(0, BLOCK), done[0][1], done[1][1]).astype(dv_ref.dtype)
    dq_ref[...] = (dq_acc[...] * SCALE).astype(dq_ref.dtype)


def block_bounds(q_seg, k_seg):
    def ranges(mine, other):
        first = mine[:, ::BLOCK][:, :, None]
        last = mine[:, BLOCK - 1::BLOCK][:, :, None]
        low = jnp.sum((other[:, None, :] < first).astype(jnp.int32), axis=-1) // BLOCK
        high = (jnp.sum((other[:, None, :] <= last).astype(jnp.int32), axis=-1) + BLOCK - 1) // BLOCK
        return low, jnp.maximum(high, low)

    wide = k_seg.shape[1] // BLOCK

    def pad(table):
        return jnp.pad(table, ((0, 0), (0, wide - table.shape[1])))

    kl, kh = ranges(q_seg, k_seg)
    ql, qh = ranges(k_seg, q_seg)
    return jnp.stack([pad(kl), pad(kh), pad(ql), pad(qh)], axis=1)


def doc_marks(segments, far):
    lane = lax.broadcasted_iota(jnp.int32, segments.shape + (PAIR,), segments.ndim) % HEAD_DIM
    own = lane == segments[..., None]
    docs = lane < 4
    if far:
        return jnp.where(docs & ~own, -FAR, 0.0).astype(jnp.bfloat16)
    return jnp.where(own, FAR, 0.0).astype(jnp.bfloat16)


def specs(rows):
    own = pl.BlockSpec((None, rows, PAIR), lambda s, p, b: (p, s, 0))
    shared = pl.BlockSpec((None, rows, PAIR), lambda s, p, b: (s, 0, 0))
    return own, shared


def attend(q, k, v, q_mark, k_mark, bounds):
    pairs, seqs = q.shape[0], q_mark.shape[0]
    rows = q.shape[1] // seqs
    q_spec, qm_spec = specs(rows)
    k_spec, km_spec = specs(LEN)
    lse_spec = pl.BlockSpec((None, None, 2, rows), lambda s, p, b: (s, p, 0, 0))
    return pl.pallas_call(
        attend_kernel,
        grid_spec=pltpu.PrefetchScalarGridSpec(
            num_scalar_prefetch=1,
            grid=(seqs, pairs),
            in_specs=[q_spec, k_spec, k_spec, qm_spec, km_spec],
            out_specs=[q_spec, lse_spec],
        ),
        out_shape=[
            jax.ShapeDtypeStruct(q.shape, jnp.bfloat16),
            jax.ShapeDtypeStruct((seqs, pairs, 2, rows), jnp.float32),
        ],
        cost_estimate=pl.CostEstimate(
            flops=8 * q.size * LEN, bytes_accessed=12 * k.size, transcendentals=2 * rows * LEN * pairs
        ),
        name="attend",
    )(bounds, q, k, v, q_mark, k_mark)


def attend_back(q, k, v, q_mark, k_mark, bounds, lse, o, do, kv_type):
    pairs, seqs = q.shape[0], q_mark.shape[0]
    rows = q.shape[1] // seqs
    q_spec, qm_spec = specs(rows)
    k_spec, km_spec = specs(LEN)
    lse_spec = pl.BlockSpec((None, None, 2, rows), lambda s, p, b: (s, p, 0, 0))
    return pl.pallas_call(
        attend_back_kernel,
        grid_spec=pltpu.PrefetchScalarGridSpec(
            num_scalar_prefetch=1,
            grid=(seqs, pairs),
            in_specs=[q_spec, k_spec, k_spec, qm_spec, km_spec, lse_spec, q_spec, q_spec],
            out_specs=[q_spec, k_spec, k_spec],
            scratch_shapes=[pltpu.VMEM((rows, PAIR), jnp.float32), pltpu.VMEM((2, rows), jnp.float32)],
        ),
        out_shape=[
            jax.ShapeDtypeStruct(q.shape, kv_type),
            jax.ShapeDtypeStruct(k.shape, kv_type),
            jax.ShapeDtypeStruct(k.shape, kv_type),
        ],
        cost_estimate=pl.CostEstimate(
            flops=20 * q.size * LEN, bytes_accessed=24 * k.size, transcendentals=2 * rows * LEN * pairs
        ),
        name="attend_back",
    )(bounds, q, k, v, q_mark, k_mark, lse, o, do)


def gather_blocks(weight):
    blocks = lax.all_gather(weight, OWNERS, axis=0, tiled=False)
    return blocks.reshape((lax.axis_size("shard"), lax.axis_size("tensor")) + weight.shape)


def pair_blocks(blocks):
    shards, _, three, rows, cols = blocks.shape
    if cols == PAIR:
        return blocks
    columns = blocks.transpose(0, 2, 3, 1, 4).reshape(shards, three, rows, -1, PAIR)
    return columns.transpose(0, 3, 1, 2, 4)


def unpair_blocks(blocks, tensors):
    shards, pairs, four, _, rows = blocks.shape
    if pairs == tensors:
        return blocks
    split = blocks.reshape(shards, pairs, four, tensors // pairs, -1, rows)
    return split.transpose(0, 1, 3, 2, 4, 5)


def scatter_blocks(blocks, block_shape):
    flat = blocks.reshape(-1, block_shape[-1])
    flat = with_layout_constraint(flat, Layout(major_to_minor=(0, 1)))
    owned = lax.psum_scatter(flat, OWNERS, scatter_dimension=0, tiled=True)
    owned = with_layout_constraint(owned, Layout(major_to_minor=(0, 1)))
    return owned.reshape(block_shape)


def over_replicas(owned):
    count = lax.axis_size("replica")
    total = owned.astype(jnp.float32)
    for step in range(1, count):
        ring = [(i, (i + step) % count) for i in range(count)]
        total = total + lax.ppermute(owned, "replica", ring).astype(jnp.float32)
    return total


def sum_over(values, axis):
    count = lax.axis_size(axis)
    if count & (count - 1):
        return lax.psum(values, axis)
    step = 1
    while step < count:
        values = values + lax.ppermute(values, axis, [(i, i ^ step) for i in range(count)])
        step *= 2
    return values


def dot(spec, left, right):
    return jnp.einsum(spec, left, right, preferred_element_type=jnp.float32)


def mean_of(values):
    return jnp.mean(values, axis=(0, 2), keepdims=True)


def normalize(residual, gain_vec, shift_vec):
    center = residual - mean_of(residual)
    spread = lax.rsqrt(mean_of(center * center) + EPSILON)
    normed = center * spread
    return (normed * gain_vec + shift_vec, normed, spread)


def norm_back(incoming, normed, spread, gain_vec):
    scaled = incoming * gain_vec
    back_grad = spread * (scaled - mean_of(scaled) - normed * mean_of(scaled * normed))
    return (back_grad, jnp.sum(incoming * normed, axis=1), jnp.sum(incoming, axis=1))


def layer(
    layer_input,
    segment_ids,
    qkv_weight,
    qkv_bias,
    out_weight,
    out_bias,
    norm1_gain,
    norm1_bias,
    up_weight,
    up_bias,
    down_weight,
    down_bias,
    norm2_gain,
    norm2_bias,
    output_grad,
):
    rows, width = layer_input.shape
    tensor_index = lax.axis_index("tensor")
    tensors = lax.axis_size("tensor")
    shards = lax.axis_size("shard")
    pairs = width // PAIR
    sharers = max(1, LEN // rows)
    seqs_here = max(1, rows // LEN)
    query_rows = min(rows, LEN)
    sharing = [list(range(i, i + sharers)) for i in range(0, tensors, sharers)]

    w_attn = gather_blocks(jnp.concatenate([qkv_weight, out_weight.T[None]]))
    w_up = gather_blocks(up_weight)
    w_down = gather_blocks(down_weight)
    w_attn = pair_blocks(w_attn)
    w_qkv, w_out = w_attn[:, :, :3], w_attn[:, :, 3]
    biases = lax.all_gather(
        jnp.concatenate([qkv_bias[0], qkv_bias[1], up_bias]), "tensor", axis=0, tiled=False
    )
    width_here, hidden_here = qkv_bias.shape[1], up_bias.shape[0]
    bias_q = biases[:, :width_here].reshape(pairs, 1, PAIR)
    bias_v = biases[:, width_here : 2 * width_here].reshape(pairs, 1, PAIR)
    bias_up = biases[:, 2 * width_here :].reshape(tensors, 1, hidden_here)

    def vec(values):
        return values.reshape(shards, 1, width // shards)

    def halves(rows_array):
        return rows_array.reshape(rows, shards, width // shards).transpose(1, 0, 2)

    def whole(blocks):
        return blocks.transpose(1, 0, 2).reshape(rows, width)

    first_seq = tensor_index * rows // LEN
    key_segments = lax.dynamic_slice_in_dim(segment_ids, first_seq, seqs_here, 0)
    query_start = tensor_index * rows % LEN
    query_segments = lax.dynamic_slice_in_dim(key_segments, query_start, query_rows, 1)
    bounds = block_bounds(query_segments, key_segments)
    q_mark, k_mark = doc_marks(query_segments, True), doc_marks(key_segments, False)

    def whole_rows(rows_array):
        if sharers == 1:
            return rows_array
        return lax.all_gather(rows_array, "tensor", axis_index_groups=sharing, axis=1, tiled=True)

    def own_rows(rows_array):
        if sharers == 1:
            return rows_array
        return lax.psum_scatter(
            rows_array, "tensor", axis_index_groups=sharing, scatter_dimension=1, tiled=True
        )

    tokens = halves(layer_input)
    projected = dot("std,snjdc->jntc", tokens, w_qkv)
    queries = ((projected[0] + bias_q).astype(jnp.bfloat16) * SCALE).astype(jnp.bfloat16)
    key_rows = whole_rows(projected[1].astype(jnp.bfloat16))
    value_rows = whole_rows((projected[2] + bias_v).astype(jnp.bfloat16))
    mixed, log_total = attend(queries, key_rows, value_rows, q_mark, k_mark, bounds)
    residual_one = tokens.astype(jnp.float32) + dot("ntc,sndc->std", mixed, w_out) + vec(out_bias)
    hidden_one, normed_one, spread_one = normalize(residual_one, vec(norm1_gain), vec(norm1_bias))
    hidden_low = hidden_one.astype(jnp.bfloat16)
    pre_act = dot("std,sndf->ntf", hidden_low, w_up) + bias_up
    normal_cdf = 0.5 * (1.0 + lax.erf(pre_act * (1.0 / math.sqrt(2.0))))
    normal_pdf = jnp.exp(-0.5 * pre_act * pre_act) * (1.0 / math.sqrt(2.0 * math.pi))
    activ = (pre_act * normal_cdf).astype(jnp.bfloat16)
    slope = (normal_cdf + pre_act * normal_pdf).astype(jnp.bfloat16)
    activ, slope = lax.optimization_barrier((activ, slope))
    residual_two = hidden_one + dot("ntf,snfd->std", activ, w_down) + vec(down_bias)
    final_out, normed_two, spread_two = normalize(residual_two, vec(norm2_gain), vec(norm2_bias))
    resid_two_grad, gain_two_grad, shift_two_grad = norm_back(
        halves(output_grad).astype(jnp.float32), normed_two, spread_two, vec(norm2_gain)
    )
    down_bias_part = jnp.sum(resid_two_grad, axis=1)
    branch_grad = resid_two_grad.astype(jnp.bfloat16)
    down_grad = dot("ntf,std->sndf", activ, branch_grad).astype(jnp.bfloat16)
    down_owned = scatter_blocks(down_grad, down_weight.shape[::-1])
    activ_grad = dot("std,snfd->ntf", branch_grad, w_down)
    pre_grad = activ_grad * slope.astype(jnp.float32)
    up_bias_part = jnp.sum(pre_grad, axis=1)
    pre_low = pre_grad.astype(jnp.bfloat16)
    up_grad = dot("ntf,std->sndf", pre_low, hidden_low).astype(jnp.bfloat16)
    up_owned = scatter_blocks(up_grad, up_weight.shape)
    back_middle = dot("ntf,sndf->std", pre_low, w_up)
    resid_one_grad, gain_one_grad, shift_one_grad = norm_back(
        resid_two_grad + back_middle, normed_one, spread_one, vec(norm1_gain)
    )
    out_bias_part = jnp.sum(resid_one_grad, axis=1)
    attn_grad = resid_one_grad.astype(jnp.bfloat16)
    out_grad = dot("ntc,std->sncd", mixed, attn_grad).astype(jnp.bfloat16)
    mixed_grad = dot("std,sndc->ntc", attn_grad, w_out).astype(jnp.bfloat16)
    grad_type = jnp.bfloat16 if sharers == 1 else jnp.float32
    query_grad, key_grad, value_grad = attend_back(
        queries, key_rows, value_rows, q_mark, k_mark, bounds, log_total, mixed, mixed_grad, grad_type
    )
    key_grad, value_grad = own_rows(key_grad), own_rows(value_grad)
    proj_low = jnp.stack([query_grad, key_grad, value_grad]).astype(jnp.bfloat16)
    qkv_grad = [dot("ntc,std->sncd", proj_low[j], tokens).astype(jnp.bfloat16) for j in range(3)]
    attn_weight_grad = jnp.stack(qkv_grad + [out_grad], axis=2)
    attn_owned = scatter_blocks(
        unpair_blocks(attn_weight_grad, tensors), (4,) + out_weight.shape
    )
    back_input = dot("jntc,snjdc->std", proj_low, w_qkv)
    input_grad = resid_one_grad + back_input
    down_owned = over_replicas(down_owned).T
    up_owned = over_replicas(up_owned)
    attn_owned = over_replicas(attn_owned)
    qkv_owned, out_owned = attn_owned[:3].transpose(0, 2, 1), attn_owned[3]
    parts = (
        jnp.sum(query_grad.astype(jnp.float32), axis=1),
        jnp.sum(value_grad.astype(jnp.float32), axis=1),
        up_bias_part,
        out_bias_part,
        gain_one_grad,
        shift_one_grad,
        down_bias_part,
        gain_two_grad,
        shift_two_grad,
    )
    parts = [part.reshape(-1) for part in parts]
    summed = jnp.concatenate(parts).reshape(-1, PAIR)
    for axis in EVERYONE:
        summed = sum_over(summed, axis)
    summed = summed.reshape(-1)
    ends = [0]
    for part in parts:
        ends.append(ends[-1] + part.shape[0])
    summed = [summed[ends[i] : ends[i + 1]] for i in range(len(parts))]
    qkv_bias_grad = lax.dynamic_slice_in_dim(
        jnp.stack(summed[:2]), tensor_index * width_here, width_here, 1
    )
    up_bias_grad = lax.dynamic_slice_in_dim(summed[2], tensor_index * hidden_here, hidden_here, 0)
    return (
        whole(final_out.astype(jnp.bfloat16)),
        whole(input_grad),
        qkv_owned,
        qkv_bias_grad,
        out_owned,
        summed[3],
        summed[4],
        summed[5],
        up_owned,
        up_bias_grad,
        down_owned,
        summed[6],
        summed[7],
        summed[8],
    )


def solution(mesh):
    placed = (
        P(("replica", "shard", "tensor"), None),
        P(("replica", "shard"), None),
        P(None, "shard", "tensor"),
        P(None, "tensor"),
        P("tensor", "shard"),
        P(),
        P(),
        P(),
        P("shard", "tensor"),
        P("tensor"),
        P("tensor", "shard"),
        P(),
        P(),
        P(),
        P(("replica", "shard", "tensor"), None),
    )
    return jax.shard_map(
        layer,
        mesh=mesh,
        in_specs=placed,
        out_specs=(
            P(("replica", "shard", "tensor"), None),
            P(("replica", "shard", "tensor"), None),
            P(None, "shard", "tensor"),
            P(None, "tensor"),
            P("tensor", "shard"),
            P(),
            P(),
            P(),
            P("shard", "tensor"),
            P("tensor"),
            P("tensor", "shard"),
            P(),
            P(),
            P(),
        ),
        check_vma=False,
    )
```

```python
import jax
import jax.numpy as jnp
from jax import lax
from jax.experimental.layout import Layout, with_layout_constraint
from jax.experimental import pallas as pl
from jax.experimental.pallas import tpu as pltpu
from jax.sharding import PartitionSpec as P


import math

HEAD_DIM = 64
LEN = 1024
BLOCK = 256
PAIR = 128
FAR = 1e15
SCALE = HEAD_DIM ** (-0.5)
EPSILON = 1e-05
OWNERS = ("shard", "tensor")
EVERYONE = ("replica", "shard", "tensor")


def lanes_of(head, rows):
    lane = lax.broadcasted_iota(jnp.int32, (rows, PAIR), 1)
    return (lane // HEAD_DIM) == head


def with_marks(rows_block, marks, head):
    return jnp.where(lanes_of(head, rows_block.shape[0]), rows_block, marks)


def only_head(rows_block, head):
    return jnp.where(lanes_of(head, rows_block.shape[0]), rows_block, jnp.zeros_like(rows_block))


def attend_kernel(bounds, q_ref, k_ref, v_ref, qmark_ref, kmark_ref, o_ref, lse_ref):
    s_id = pl.program_id(0)
    blocks = q_ref.shape[0] // BLOCK
    for qb in range(blocks):
        rows = slice(qb * BLOCK, (qb + 1) * BLOCK)
        q = q_ref[rows, :]
        qmark = qmark_ref[rows, :]
        q_aug = [with_marks(q, qmark, h) for h in range(2)]

        def step(kb, carry):
            keys = pl.ds(pl.multiple_of(kb * BLOCK, BLOCK), BLOCK)
            k = k_ref[keys, :]
            v = v_ref[keys, :]
            kmark = kmark_ref[keys, :]
            out = []
            for h in range(2):
                top, total, acc = carry[h]
                scores = lax.dot_general(q_aug[h], with_marks(k, kmark, h), (((1,), (1,)), ((), ())),
                                         preferred_element_type=jnp.float32)
                new_top = jnp.maximum(top, jnp.max(scores, axis=-1, keepdims=True))
                fade = jnp.exp(top - new_top)
                weights = jnp.exp(scores - new_top)
                total = total * fade + jnp.sum(weights, axis=-1, keepdims=True)
                acc = acc * fade + jnp.dot(weights.astype(jnp.bfloat16), v, preferred_element_type=jnp.float32)
                out.append((new_top, total, acc))
            return tuple(out)

        start = tuple((jnp.full((BLOCK, 1), -3e38, jnp.float32), jnp.zeros((BLOCK, 1), jnp.float32),
                       jnp.zeros((BLOCK, PAIR), jnp.float32)) for _ in range(2))
        done = lax.fori_loop(bounds[s_id, 0, qb], bounds[s_id, 1, qb], step, start)
        (m0, l0, a0), (m1, l1, a1) = done
        o_ref[rows, :] = jnp.where(lanes_of(0, BLOCK), a0 / l0, a1 / l1).astype(o_ref.dtype)
        lse = jnp.where(lanes_of(0, BLOCK), m0 + jnp.log(l0), m1 + jnp.log(l1))
        flat = jnp.transpose(lse)
        lse_ref[0:1, rows] = flat[0:1, :]
        lse_ref[1:2, rows] = flat[HEAD_DIM:HEAD_DIM + 1, :]


def attend_back_kernel(bounds, q_ref, k_ref, v_ref, qmark_ref, kmark_ref, lse_ref, o_ref, do_ref,
                       dq_ref, dk_ref, dv_ref, dq_acc, delta_acc):
    s_id = pl.program_id(0)
    q_blocks = q_ref.shape[0] // BLOCK
    dq_acc[...] = jnp.zeros_like(dq_acc)
    for qb in range(q_blocks):
        rows = slice(qb * BLOCK, (qb + 1) * BLOCK)
        prod = do_ref[rows, :].astype(jnp.float32) * o_ref[rows, :].astype(jnp.float32)
        flat = jnp.transpose(prod)
        delta_acc[0:1, rows] = jnp.sum(flat[:HEAD_DIM, :], axis=0, keepdims=True)
        delta_acc[1:2, rows] = jnp.sum(flat[HEAD_DIM:, :], axis=0, keepdims=True)
    for kb in range(k_ref.shape[0] // BLOCK):
        keys = slice(kb * BLOCK, (kb + 1) * BLOCK)
        k = k_ref[keys, :]
        v = v_ref[keys, :]
        kmark = kmark_ref[keys, :]
        k_aug = [with_marks(k, kmark, h) for h in range(2)]
        v_own = [only_head(v, h) for h in range(2)]

        def step(qb, carry):
            rows = pl.ds(pl.multiple_of(qb * BLOCK, BLOCK), BLOCK)
            q = q_ref[rows, :]
            do = do_ref[rows, :]
            qmark = qmark_ref[rows, :]
            out, dq_parts = [], []
            for h in range(2):
                dk, dv = carry[h]
                scores = lax.dot_general(k_aug[h], with_marks(q, qmark, h), (((1,), (1,)), ((), ())),
                                         preferred_element_type=jnp.float32)
                probs = jnp.exp(scores - lse_ref[h:h + 1, rows])
                prob_grad = lax.dot_general(v_own[h], do, (((1,), (1,)), ((), ())),
                                            preferred_element_type=jnp.float32)
                score_low = (probs * (prob_grad - delta_acc[h:h + 1, rows])).astype(jnp.bfloat16)
                dv = dv + jnp.dot(probs.astype(jnp.bfloat16), do, preferred_element_type=jnp.float32)
                dk = dk + jnp.dot(score_low, q, preferred_element_type=jnp.float32)
                dq_parts.append(lax.dot_general(score_low, k, (((0,), (0,)), ((), ())),
                                                preferred_element_type=jnp.float32))
                out.append((dk, dv))
            dq_acc[rows, :] += jnp.where(lanes_of(0, BLOCK), dq_parts[0], dq_parts[1])
            return tuple(out)

        zero = jnp.zeros((BLOCK, PAIR), jnp.float32)
        done = lax.fori_loop(bounds[s_id, 2, kb], bounds[s_id, 3, kb], step, ((zero, zero), (zero, zero)))
        dk_ref[keys, :] = jnp.where(lanes_of(0, BLOCK), done[0][0], done[1][0]).astype(dk_ref.dtype)
        dv_ref[keys, :] = jnp.where(lanes_of(0, BLOCK), done[0][1], done[1][1]).astype(dv_ref.dtype)
    dq_ref[...] = (dq_acc[...] * SCALE).astype(dq_ref.dtype)


def block_bounds(q_seg, k_seg):
    def ranges(mine, other):
        first = mine[:, ::BLOCK][:, :, None]
        last = mine[:, BLOCK - 1::BLOCK][:, :, None]
        low = jnp.sum((other[:, None, :] < first).astype(jnp.int32), axis=-1) // BLOCK
        high = (jnp.sum((other[:, None, :] <= last).astype(jnp.int32), axis=-1) + BLOCK - 1) // BLOCK
        return low, jnp.maximum(high, low)

    wide = k_seg.shape[1] // BLOCK

    def pad(table):
        return jnp.pad(table, ((0, 0), (0, wide - table.shape[1])))

    kl, kh = ranges(q_seg, k_seg)
    ql, qh = ranges(k_seg, q_seg)
    return jnp.stack([pad(kl), pad(kh), pad(ql), pad(qh)], axis=1)


def doc_marks(segments, far):
    lane = lax.broadcasted_iota(jnp.int32, segments.shape + (PAIR,), segments.ndim) % HEAD_DIM
    own = lane == segments[..., None]
    docs = lane < 4
    if far:
        return jnp.where(docs & ~own, -FAR, 0.0).astype(jnp.bfloat16)
    return jnp.where(own, FAR, 0.0).astype(jnp.bfloat16)


def specs(rows):
    own = pl.BlockSpec((None, rows, PAIR), lambda s, p, b: (p, s, 0))
    shared = pl.BlockSpec((None, rows, PAIR), lambda s, p, b: (s, 0, 0))
    return own, shared


def attend(q, k, v, q_mark, k_mark, bounds):
    pairs, seqs = q.shape[0], q_mark.shape[0]
    rows = q.shape[1] // seqs
    q_spec, qm_spec = specs(rows)
    k_spec, km_spec = specs(LEN)
    lse_spec = pl.BlockSpec((None, None, 2, rows), lambda s, p, b: (s, p, 0, 0))
    return pl.pallas_call(
        attend_kernel,
        grid_spec=pltpu.PrefetchScalarGridSpec(
            num_scalar_prefetch=1,
            grid=(seqs, pairs),
            in_specs=[q_spec, k_spec, k_spec, qm_spec, km_spec],
            out_specs=[q_spec, lse_spec],
        ),
        out_shape=[
            jax.ShapeDtypeStruct(q.shape, jnp.bfloat16),
            jax.ShapeDtypeStruct((seqs, pairs, 2, rows), jnp.float32),
        ],
        cost_estimate=pl.CostEstimate(
            flops=8 * q.size * LEN, bytes_accessed=12 * k.size, transcendentals=2 * rows * LEN * pairs
        ),
        name="attend",
    )(bounds, q, k, v, q_mark, k_mark)


def attend_back(q, k, v, q_mark, k_mark, bounds, lse, o, do, kv_type, first, count):
    seqs = q_mark.shape[0]
    rows = q.shape[1] // seqs

    def own(length):
        return pl.BlockSpec((None, length, PAIR), lambda s, p, b: (p + first, s, 0))

    def result(length):
        return pl.BlockSpec((None, length, PAIR), lambda s, p, b: (p, s, 0))

    _, qm_spec = specs(rows)
    _, km_spec = specs(LEN)
    lse_spec = pl.BlockSpec((None, None, 2, rows), lambda s, p, b: (s, p + first, 0, 0))
    return pl.pallas_call(
        attend_back_kernel,
        grid_spec=pltpu.PrefetchScalarGridSpec(
            num_scalar_prefetch=1,
            grid=(seqs, count),
            in_specs=[own(rows), own(LEN), own(LEN), qm_spec, km_spec, lse_spec, own(rows), own(rows)],
            out_specs=[result(rows), result(LEN), result(LEN)],
            scratch_shapes=[pltpu.VMEM((rows, PAIR), jnp.float32), pltpu.VMEM((2, rows), jnp.float32)],
        ),
        out_shape=[
            jax.ShapeDtypeStruct((count,) + q.shape[1:], kv_type),
            jax.ShapeDtypeStruct((count,) + k.shape[1:], kv_type),
            jax.ShapeDtypeStruct((count,) + k.shape[1:], kv_type),
        ],
        cost_estimate=pl.CostEstimate(
            flops=20 * count * rows * seqs * PAIR * LEN,
            bytes_accessed=24 * count * k.shape[1] * PAIR,
            transcendentals=2 * rows * LEN * count * seqs,
        ),
        name="attend_back",
    )(bounds, q, k, v, q_mark, k_mark, lse, o, do)


def gather_blocks(weight):
    blocks = lax.all_gather(weight, OWNERS, axis=0, tiled=False)
    return blocks.reshape((lax.axis_size("shard"), lax.axis_size("tensor")) + weight.shape)


def pair_blocks(blocks):
    shards, _, three, rows, cols = blocks.shape
    if cols == PAIR:
        return blocks
    columns = blocks.transpose(0, 2, 3, 1, 4).reshape(shards, three, rows, -1, PAIR)
    return columns.transpose(0, 3, 1, 2, 4)


def unpair_blocks(blocks, tensors):
    shards, pairs, four, _, rows = blocks.shape
    if pairs == tensors:
        return blocks
    split = blocks.reshape(shards, pairs, four, tensors // pairs, -1, rows)
    return split.transpose(0, 1, 3, 2, 4, 5)


def scatter_blocks(blocks, block_shape):
    flat = blocks.reshape(-1, block_shape[-1])
    flat = with_layout_constraint(flat, Layout(major_to_minor=(0, 1)))
    owned = lax.psum_scatter(flat, OWNERS, scatter_dimension=0, tiled=True)
    owned = with_layout_constraint(owned, Layout(major_to_minor=(0, 1)))
    return owned.reshape(block_shape)


def fold_replicas(blocks):
    count, me = lax.axis_size("replica"), lax.axis_index("replica")
    owners, rows, cols = blocks.shape
    parts = blocks.reshape(owners, count, rows // count, cols)
    total = lax.dynamic_index_in_dim(parts, me, 1, keepdims=False).astype(jnp.float32)
    for step in range(1, count):
        ring = [(i, (i + step) % count) for i in range(count)]
        sent = lax.dynamic_index_in_dim(parts, (me + step) % count, 1, keepdims=False)
        total = total + lax.ppermute(sent, "replica", ring).astype(jnp.float32)
    return total.astype(jnp.bfloat16)


def unfold_replicas(owned):
    count, me = lax.axis_size("replica"), lax.axis_index("replica")
    arrived = [owned]
    for step in range(1, count):
        ring = [(i, (i + step) % count) for i in range(count)]
        arrived.append(lax.ppermute(owned, "replica", ring))
    arrived = jnp.stack(arrived).astype(jnp.float32)
    parts = [
        lax.dynamic_index_in_dim(arrived, (me - k) % count, 0, keepdims=False) for k in range(count)
    ]
    return jnp.concatenate(parts, axis=0)


def over_replicas(owned):
    count = lax.axis_size("replica")
    total = owned.astype(jnp.float32)
    for step in range(1, count):
        ring = [(i, (i + step) % count) for i in range(count)]
        total = total + lax.ppermute(owned, "replica", ring).astype(jnp.float32)
    return total


def sum_over(values, axis):
    count = lax.axis_size(axis)
    if count & (count - 1):
        return lax.psum(values, axis)
    step = 1
    while step < count:
        values = values + lax.ppermute(values, axis, [(i, i ^ step) for i in range(count)])
        step *= 2
    return values


def dot(spec, left, right):
    return jnp.einsum(spec, left, right, preferred_element_type=jnp.float32)


def mean_of(values):
    return jnp.mean(values, axis=(0, 2), keepdims=True)


def normalize(residual, gain_vec, shift_vec):
    center = residual - mean_of(residual)
    spread = lax.rsqrt(mean_of(center * center) + EPSILON)
    normed = center * spread
    return (normed * gain_vec + shift_vec, normed, spread)


def norm_back(incoming, normed, spread, gain_vec):
    scaled = incoming * gain_vec
    back_grad = spread * (scaled - mean_of(scaled) - normed * mean_of(scaled * normed))
    return (back_grad, jnp.sum(incoming * normed, axis=1), jnp.sum(incoming, axis=1))


def layer(
    layer_input,
    segment_ids,
    qkv_weight,
    qkv_bias,
    out_weight,
    out_bias,
    norm1_gain,
    norm1_bias,
    up_weight,
    up_bias,
    down_weight,
    down_bias,
    norm2_gain,
    norm2_bias,
    output_grad,
):
    rows, width = layer_input.shape
    tensor_index = lax.axis_index("tensor")
    tensors = lax.axis_size("tensor")
    shards = lax.axis_size("shard")
    pairs = width // PAIR
    sharers = max(1, LEN // rows)
    seqs_here = max(1, rows // LEN)
    query_rows = min(rows, LEN)
    sharing = [list(range(i, i + sharers)) for i in range(0, tensors, sharers)]

    w_attn = gather_blocks(jnp.concatenate([qkv_weight, out_weight.T[None]]))
    w_up = gather_blocks(up_weight)
    w_down = gather_blocks(down_weight)
    w_attn = pair_blocks(w_attn)
    w_qkv, w_out = w_attn[:, :, :3], w_attn[:, :, 3]
    biases = lax.all_gather(
        jnp.concatenate([qkv_bias[0], qkv_bias[1], up_bias]), "tensor", axis=0, tiled=False
    )
    width_here, hidden_here = qkv_bias.shape[1], up_bias.shape[0]
    bias_q = biases[:, :width_here].reshape(pairs, 1, PAIR)
    bias_v = biases[:, width_here : 2 * width_here].reshape(pairs, 1, PAIR)
    bias_up = biases[:, 2 * width_here :].reshape(tensors, 1, hidden_here)

    def vec(values):
        return values.reshape(shards, 1, width // shards)

    def halves(rows_array):
        return rows_array.reshape(rows, shards, width // shards).transpose(1, 0, 2)

    def whole(blocks):
        return blocks.transpose(1, 0, 2).reshape(rows, width)

    first_seq = tensor_index * rows // LEN
    key_segments = lax.dynamic_slice_in_dim(segment_ids, first_seq, seqs_here, 0)
    query_start = tensor_index * rows % LEN
    query_segments = lax.dynamic_slice_in_dim(key_segments, query_start, query_rows, 1)
    bounds = block_bounds(query_segments, key_segments)
    q_mark, k_mark = doc_marks(query_segments, True), doc_marks(key_segments, False)

    def whole_rows(rows_array):
        if sharers == 1:
            return rows_array
        return lax.all_gather(rows_array, "tensor", axis_index_groups=sharing, axis=1, tiled=True)

    def own_rows(rows_array):
        if sharers == 1:
            return rows_array
        return lax.psum_scatter(
            rows_array, "tensor", axis_index_groups=sharing, scatter_dimension=1, tiled=True
        )

    tokens = halves(layer_input)
    projected = dot("std,snjdc->jntc", tokens, w_qkv)
    queries = ((projected[0] + bias_q).astype(jnp.bfloat16) * SCALE).astype(jnp.bfloat16)
    key_rows = whole_rows(projected[1].astype(jnp.bfloat16))
    value_rows = whole_rows((projected[2] + bias_v).astype(jnp.bfloat16))
    mixed, log_total = attend(queries, key_rows, value_rows, q_mark, k_mark, bounds)
    residual_one = tokens.astype(jnp.float32) + dot("ntc,sndc->std", mixed, w_out) + vec(out_bias)
    hidden_one, normed_one, spread_one = normalize(residual_one, vec(norm1_gain), vec(norm1_bias))
    hidden_low = hidden_one.astype(jnp.bfloat16)
    pre_act = dot("std,sndf->ntf", hidden_low, w_up) + bias_up
    normal_cdf = 0.5 * (1.0 + lax.erf(pre_act * (1.0 / math.sqrt(2.0))))
    normal_pdf = jnp.exp(-0.5 * pre_act * pre_act) * (1.0 / math.sqrt(2.0 * math.pi))
    activ = (pre_act * normal_cdf).astype(jnp.bfloat16)
    slope = (normal_cdf + pre_act * normal_pdf).astype(jnp.bfloat16)
    activ, slope = lax.optimization_barrier((activ, slope))
    residual_two = hidden_one + dot("ntf,snfd->std", activ, w_down) + vec(down_bias)
    final_out, normed_two, spread_two = normalize(residual_two, vec(norm2_gain), vec(norm2_bias))
    resid_two_grad, gain_two_grad, shift_two_grad = norm_back(
        halves(output_grad).astype(jnp.float32), normed_two, spread_two, vec(norm2_gain)
    )
    down_bias_part = jnp.sum(resid_two_grad, axis=1)
    branch_grad = resid_two_grad.astype(jnp.bfloat16)
    down_grad = dot("ntf,std->sndf", activ, branch_grad).astype(jnp.bfloat16)
    down_owned = scatter_blocks(down_grad, down_weight.shape[::-1])
    activ_grad = dot("std,snfd->ntf", branch_grad, w_down)
    pre_grad = activ_grad * slope.astype(jnp.float32)
    up_bias_part = jnp.sum(pre_grad, axis=1)
    pre_low = pre_grad.astype(jnp.bfloat16)
    up_grad = dot("ntf,std->sndf", pre_low, hidden_low).astype(jnp.bfloat16)
    owners = shards * tensors
    up_folded = fold_replicas(up_grad.reshape((owners,) + up_weight.shape))
    up_owned = scatter_blocks(up_folded, up_folded.shape[1:])
    back_middle = dot("ntf,sndf->std", pre_low, w_up)
    resid_one_grad, gain_one_grad, shift_one_grad = norm_back(
        resid_two_grad + back_middle, normed_one, spread_one, vec(norm1_gain)
    )
    out_bias_part = jnp.sum(resid_one_grad, axis=1)
    attn_grad = resid_one_grad.astype(jnp.bfloat16)
    out_grad = dot("ntc,std->sncd", mixed, attn_grad).astype(jnp.bfloat16)
    mixed_grad = dot("std,sndc->ntc", attn_grad, w_out).astype(jnp.bfloat16)
    grad_type = jnp.bfloat16 if sharers == 1 else jnp.float32
    half = pairs // 2
    grads = []
    for first, count in ((0, half), (half, pairs - half)):
        grads.append(
            attend_back(
                queries,
                key_rows,
                value_rows,
                q_mark,
                k_mark,
                bounds,
                log_total,
                mixed,
                mixed_grad,
                grad_type,
                first,
                count,
            )
        )
    query_grad, key_grad, value_grad = [jnp.concatenate(both) for both in zip(*grads)]
    key_grad, value_grad = own_rows(key_grad), own_rows(value_grad)
    proj_low = jnp.stack([query_grad, key_grad, value_grad]).astype(jnp.bfloat16)

    def weight_grad(j):
        return dot("ntc,std->sncd", proj_low[j], tokens).astype(jnp.bfloat16)

    def by_owner(grads):
        blocks = unpair_blocks(jnp.stack(grads, axis=2), tensors)
        return blocks.reshape(owners, -1, width // shards)

    query_key_grad = by_owner([weight_grad(0), weight_grad(1)])
    query_key_folded = fold_replicas(query_key_grad)
    value_out_grad = by_owner([weight_grad(2), out_grad])
    value_out_owned = scatter_blocks(value_out_grad, (2,) + out_weight.shape)
    down_owned = over_replicas(down_owned).T
    up_owned = unfold_replicas(up_owned)
    query_key_folded, down_owned, up_owned = lax.optimization_barrier(
        (query_key_folded, down_owned, up_owned)
    )
    query_key_owned = scatter_blocks(query_key_folded, query_key_folded.shape[1:])
    back_input = dot("jntc,snjdc->std", proj_low, w_qkv)
    input_grad = resid_one_grad + back_input
    query_key_owned = unfold_replicas(query_key_owned).reshape((2,) + out_weight.shape)
    value_owned, out_owned = over_replicas(value_out_owned)
    qkv_owned = jnp.concatenate([query_key_owned, value_owned[None]]).transpose(0, 2, 1)
    parts = (
        jnp.sum(query_grad.astype(jnp.float32), axis=1),
        jnp.sum(value_grad.astype(jnp.float32), axis=1),
        up_bias_part,
        out_bias_part,
        gain_one_grad,
        shift_one_grad,
        down_bias_part,
        gain_two_grad,
        shift_two_grad,
    )
    parts = [part.reshape(-1) for part in parts]
    summed = jnp.concatenate(parts).reshape(-1, PAIR)
    for axis in EVERYONE:
        summed = sum_over(summed, axis)
    summed = summed.reshape(-1)
    ends = [0]
    for part in parts:
        ends.append(ends[-1] + part.shape[0])
    summed = [summed[ends[i] : ends[i + 1]] for i in range(len(parts))]
    qkv_bias_grad = lax.dynamic_slice_in_dim(
        jnp.stack(summed[:2]), tensor_index * width_here, width_here, 1
    )
    up_bias_grad = lax.dynamic_slice_in_dim(summed[2], tensor_index * hidden_here, hidden_here, 0)
    return (
        whole(final_out.astype(jnp.bfloat16)),
        whole(input_grad),
        qkv_owned,
        qkv_bias_grad,
        out_owned,
        summed[3],
        summed[4],
        summed[5],
        up_owned,
        up_bias_grad,
        down_owned,
        summed[6],
        summed[7],
        summed[8],
    )


def solution(mesh):
    placed = (
        P(("replica", "shard", "tensor"), None),
        P(("replica", "shard"), None),
        P(None, "shard", "tensor"),
        P(None, "tensor"),
        P("tensor", "shard"),
        P(),
        P(),
        P(),
        P("shard", "tensor"),
        P("tensor"),
        P("tensor", "shard"),
        P(),
        P(),
        P(),
        P(("replica", "shard", "tensor"), None),
    )
    return jax.shard_map(
        layer,
        mesh=mesh,
        in_specs=placed,
        out_specs=(
            P(("replica", "shard", "tensor"), None),
            P(("replica", "shard", "tensor"), None),
            P(None, "shard", "tensor"),
            P(None, "tensor"),
            P("tensor", "shard"),
            P(),
            P(),
            P(),
            P("shard", "tensor"),
            P("tensor"),
            P("tensor", "shard"),
            P(),
            P(),
            P(),
        ),
        check_vma=False,
    )
```

```python
import jax
import jax.numpy as jnp
from jax import lax
from jax.experimental.layout import Layout, with_layout_constraint
from jax.experimental import pallas as pl
from jax.experimental.pallas import tpu as pltpu
from jax.sharding import PartitionSpec as P


import math

HEAD_DIM = 64
LEN = 1024
BLOCK = 256
PAIR = 128
FAR = 1e15
SCALE = HEAD_DIM ** (-0.5)
EPSILON = 1e-05
OWNERS = ("shard", "tensor")
EVERYONE = ("replica", "shard", "tensor")


def lanes_of(head, rows):
    lane = lax.broadcasted_iota(jnp.int32, (rows, PAIR), 1)
    return (lane // HEAD_DIM) == head


def with_marks(rows_block, marks, head):
    return jnp.where(lanes_of(head, rows_block.shape[0]), rows_block, marks)


def only_head(rows_block, head):
    return jnp.where(lanes_of(head, rows_block.shape[0]), rows_block, jnp.zeros_like(rows_block))


def attend_kernel(bounds, q_ref, k_ref, v_ref, qmark_ref, kmark_ref, o_ref, lse_ref):
    s_id = pl.program_id(0)
    blocks = q_ref.shape[0] // BLOCK
    for qb in range(blocks):
        rows = slice(qb * BLOCK, (qb + 1) * BLOCK)
        q = q_ref[rows, :]
        qmark = qmark_ref[rows, :]
        q_aug = [with_marks(q, qmark, h) for h in range(2)]

        def step(kb, carry):
            keys = pl.ds(pl.multiple_of(kb * BLOCK, BLOCK), BLOCK)
            k = k_ref[keys, :]
            v = v_ref[keys, :]
            kmark = kmark_ref[keys, :]
            out = []
            for h in range(2):
                top, total, acc = carry[h]
                scores = lax.dot_general(q_aug[h], with_marks(k, kmark, h), (((1,), (1,)), ((), ())),
                                         preferred_element_type=jnp.float32)
                new_top = jnp.maximum(top, jnp.max(scores, axis=-1, keepdims=True))
                fade = jnp.exp(top - new_top)
                weights = jnp.exp(scores - new_top)
                total = total * fade + jnp.sum(weights, axis=-1, keepdims=True)
                acc = acc * fade + jnp.dot(weights.astype(jnp.bfloat16), v, preferred_element_type=jnp.float32)
                out.append((new_top, total, acc))
            return tuple(out)

        start = tuple((jnp.full((BLOCK, 1), -3e38, jnp.float32), jnp.zeros((BLOCK, 1), jnp.float32),
                       jnp.zeros((BLOCK, PAIR), jnp.float32)) for _ in range(2))
        done = lax.fori_loop(bounds[s_id, 0, qb], bounds[s_id, 1, qb], step, start)
        (m0, l0, a0), (m1, l1, a1) = done
        o_ref[rows, :] = jnp.where(lanes_of(0, BLOCK), a0 / l0, a1 / l1).astype(o_ref.dtype)
        lse = jnp.where(lanes_of(0, BLOCK), m0 + jnp.log(l0), m1 + jnp.log(l1))
        flat = jnp.transpose(lse)
        lse_ref[0:1, rows] = flat[0:1, :]
        lse_ref[1:2, rows] = flat[HEAD_DIM:HEAD_DIM + 1, :]


def attend_back_kernel(bounds, q_ref, k_ref, v_ref, qmark_ref, kmark_ref, lse_ref, o_ref, do_ref,
                       dq_ref, dk_ref, dv_ref, dq_acc, delta_acc):
    s_id = pl.program_id(0)
    q_blocks = q_ref.shape[0] // BLOCK
    dq_acc[...] = jnp.zeros_like(dq_acc)
    for qb in range(q_blocks):
        rows = slice(qb * BLOCK, (qb + 1) * BLOCK)
        prod = do_ref[rows, :].astype(jnp.float32) * o_ref[rows, :].astype(jnp.float32)
        flat = jnp.transpose(prod)
        delta_acc[0:1, rows] = jnp.sum(flat[:HEAD_DIM, :], axis=0, keepdims=True)
        delta_acc[1:2, rows] = jnp.sum(flat[HEAD_DIM:, :], axis=0, keepdims=True)
    for kb in range(k_ref.shape[0] // BLOCK):
        keys = slice(kb * BLOCK, (kb + 1) * BLOCK)
        k = k_ref[keys, :]
        v = v_ref[keys, :]
        kmark = kmark_ref[keys, :]
        k_aug = [with_marks(k, kmark, h) for h in range(2)]
        v_own = [only_head(v, h) for h in range(2)]

        def step(qb, carry):
            rows = pl.ds(pl.multiple_of(qb * BLOCK, BLOCK), BLOCK)
            q = q_ref[rows, :]
            do = do_ref[rows, :]
            qmark = qmark_ref[rows, :]
            out, dq_parts = [], []
            for h in range(2):
                dk, dv = carry[h]
                scores = lax.dot_general(k_aug[h], with_marks(q, qmark, h), (((1,), (1,)), ((), ())),
                                         preferred_element_type=jnp.float32)
                probs = jnp.exp(scores - lse_ref[h:h + 1, rows])
                prob_grad = lax.dot_general(v_own[h], do, (((1,), (1,)), ((), ())),
                                            preferred_element_type=jnp.float32)
                score_low = (probs * (prob_grad - delta_acc[h:h + 1, rows])).astype(jnp.bfloat16)
                dv = dv + jnp.dot(probs.astype(jnp.bfloat16), do, preferred_element_type=jnp.float32)
                dk = dk + jnp.dot(score_low, q, preferred_element_type=jnp.float32)
                dq_parts.append(lax.dot_general(score_low, k, (((0,), (0,)), ((), ())),
                                                preferred_element_type=jnp.float32))
                out.append((dk, dv))
            dq_acc[rows, :] += jnp.where(lanes_of(0, BLOCK), dq_parts[0], dq_parts[1])
            return tuple(out)

        zero = jnp.zeros((BLOCK, PAIR), jnp.float32)
        done = lax.fori_loop(bounds[s_id, 2, kb], bounds[s_id, 3, kb], step, ((zero, zero), (zero, zero)))
        dk_ref[keys, :] = jnp.where(lanes_of(0, BLOCK), done[0][0], done[1][0]).astype(dk_ref.dtype)
        dv_ref[keys, :] = jnp.where(lanes_of(0, BLOCK), done[0][1], done[1][1]).astype(dv_ref.dtype)
    dq_ref[...] = (dq_acc[...] * SCALE).astype(dq_ref.dtype)


def block_bounds(q_seg, k_seg):
    def ranges(mine, other):
        first = mine[:, ::BLOCK][:, :, None]
        last = mine[:, BLOCK - 1::BLOCK][:, :, None]
        low = jnp.sum((other[:, None, :] < first).astype(jnp.int32), axis=-1) // BLOCK
        high = (jnp.sum((other[:, None, :] <= last).astype(jnp.int32), axis=-1) + BLOCK - 1) // BLOCK
        return low, jnp.maximum(high, low)

    wide = k_seg.shape[1] // BLOCK

    def pad(table):
        return jnp.pad(table, ((0, 0), (0, wide - table.shape[1])))

    kl, kh = ranges(q_seg, k_seg)
    ql, qh = ranges(k_seg, q_seg)
    return jnp.stack([pad(kl), pad(kh), pad(ql), pad(qh)], axis=1)


def doc_marks(segments, far):
    lane = lax.broadcasted_iota(jnp.int32, segments.shape + (PAIR,), segments.ndim) % HEAD_DIM
    own = lane == segments[..., None]
    docs = lane < 4
    if far:
        return jnp.where(docs & ~own, -FAR, 0.0).astype(jnp.bfloat16)
    return jnp.where(own, FAR, 0.0).astype(jnp.bfloat16)


def specs(rows):
    own = pl.BlockSpec((None, rows, PAIR), lambda s, p, b: (p, s, 0))
    shared = pl.BlockSpec((None, rows, PAIR), lambda s, p, b: (s, 0, 0))
    return own, shared


def attend(q, k, v, q_mark, k_mark, bounds):
    pairs, seqs = q.shape[0], q_mark.shape[0]
    rows = q.shape[1] // seqs
    q_spec, qm_spec = specs(rows)
    k_spec, km_spec = specs(LEN)
    lse_spec = pl.BlockSpec((None, None, 2, rows), lambda s, p, b: (s, p, 0, 0))
    return pl.pallas_call(
        attend_kernel,
        grid_spec=pltpu.PrefetchScalarGridSpec(
            num_scalar_prefetch=1,
            grid=(seqs, pairs),
            in_specs=[q_spec, k_spec, k_spec, qm_spec, km_spec],
            out_specs=[q_spec, lse_spec],
        ),
        out_shape=[
            jax.ShapeDtypeStruct(q.shape, jnp.bfloat16),
            jax.ShapeDtypeStruct((seqs, pairs, 2, rows), jnp.float32),
        ],
        cost_estimate=pl.CostEstimate(
            flops=8 * q.size * LEN, bytes_accessed=12 * k.size, transcendentals=2 * rows * LEN * pairs
        ),
        name="attend",
    )(bounds, q, k, v, q_mark, k_mark)


def attend_back(q, k, v, q_mark, k_mark, bounds, lse, o, do, kv_type):
    pairs, seqs = q.shape[0], q_mark.shape[0]
    rows = q.shape[1] // seqs
    q_spec, qm_spec = specs(rows)
    k_spec, km_spec = specs(LEN)
    lse_spec = pl.BlockSpec((None, None, 2, rows), lambda s, p, b: (s, p, 0, 0))
    return pl.pallas_call(
        attend_back_kernel,
        grid_spec=pltpu.PrefetchScalarGridSpec(
            num_scalar_prefetch=1,
            grid=(seqs, pairs),
            in_specs=[q_spec, k_spec, k_spec, qm_spec, km_spec, lse_spec, q_spec, q_spec],
            out_specs=[q_spec, k_spec, k_spec],
            scratch_shapes=[pltpu.VMEM((rows, PAIR), jnp.float32), pltpu.VMEM((2, rows), jnp.float32)],
        ),
        out_shape=[
            jax.ShapeDtypeStruct(q.shape, kv_type),
            jax.ShapeDtypeStruct(k.shape, kv_type),
            jax.ShapeDtypeStruct(k.shape, kv_type),
        ],
        cost_estimate=pl.CostEstimate(
            flops=20 * q.size * LEN, bytes_accessed=24 * k.size, transcendentals=2 * rows * LEN * pairs
        ),
        name="attend_back",
    )(bounds, q, k, v, q_mark, k_mark, lse, o, do)


def grads_kernel(branch_ref, activ_ref, hidden_ref, pre_ref, o_ref):
    o_ref[0] = jnp.dot(branch_ref[...], activ_ref[...], preferred_element_type=jnp.float32).astype(o_ref.dtype)
    o_ref[1] = jnp.dot(hidden_ref[...], pre_ref[...], preferred_element_type=jnp.float32).astype(o_ref.dtype)


def feed_forward_grads(branch, activ, hidden, pre):
    shards, tokens, wide = branch.shape
    tensors, _, deep = activ.shape
    left = pl.BlockSpec((None, wide, tokens), lambda n, s: (s, 0, 0))
    right = pl.BlockSpec((None, tokens, deep), lambda n, s: (n, 0, 0))
    return pl.pallas_call(
        grads_kernel,
        grid=(tensors, shards),
        in_specs=[left, right, left, right],
        out_specs=pl.BlockSpec((None, None, 2, wide, deep), lambda n, s: (s, n, 0, 0, 0)),
        out_shape=jax.ShapeDtypeStruct((shards, tensors, 2, wide, deep), jnp.bfloat16),
        cost_estimate=pl.CostEstimate(
            flops=4 * branch.size * tensors * deep,
            bytes_accessed=4 * (branch.size + activ.size) + 4 * shards * tensors * wide * deep,
            transcendentals=0,
        ),
        name="feed_forward_grads",
    )(branch.swapaxes(1, 2), activ, hidden.swapaxes(1, 2), pre)


def gather_blocks(weight):
    blocks = lax.all_gather(weight, OWNERS, axis=0, tiled=False)
    return blocks.reshape((lax.axis_size("shard"), lax.axis_size("tensor")) + weight.shape)


def pair_blocks(blocks):
    shards, _, three, rows, cols = blocks.shape
    if cols == PAIR:
        return blocks
    columns = blocks.transpose(0, 2, 3, 1, 4).reshape(shards, three, rows, -1, PAIR)
    return columns.transpose(0, 3, 1, 2, 4)


def unpair_blocks(blocks, tensors):
    shards, pairs, four, _, rows = blocks.shape
    if pairs == tensors:
        return blocks
    split = blocks.reshape(shards, pairs, four, tensors // pairs, -1, rows)
    return split.transpose(0, 1, 3, 2, 4, 5)


def scatter_blocks(blocks, block_shape):
    flat = blocks.reshape(-1, block_shape[-1])
    flat = with_layout_constraint(flat, Layout(major_to_minor=(0, 1)))
    owned = lax.psum_scatter(flat, OWNERS, scatter_dimension=0, tiled=True)
    owned = with_layout_constraint(owned, Layout(major_to_minor=(0, 1)))
    return owned.reshape(block_shape)


def over_replicas(owned):
    count = lax.axis_size("replica")
    total = owned.astype(jnp.float32)
    for step in range(1, count):
        ring = [(i, (i + step) % count) for i in range(count)]
        total = total + lax.ppermute(owned, "replica", ring).astype(jnp.float32)
    return total


def sum_over(values, axis):
    count = lax.axis_size(axis)
    if count & (count - 1):
        return lax.psum(values, axis)
    step = 1
    while step < count:
        values = values + lax.ppermute(values, axis, [(i, i ^ step) for i in range(count)])
        step *= 2
    return values


def dot(spec, left, right):
    return jnp.einsum(spec, left, right, preferred_element_type=jnp.float32)


def mean_of(values):
    return jnp.mean(values, axis=(0, 2), keepdims=True)


def normalize(residual, gain_vec, shift_vec):
    center = residual - mean_of(residual)
    spread = lax.rsqrt(mean_of(center * center) + EPSILON)
    normed = center * spread
    return (normed * gain_vec + shift_vec, normed, spread)


def norm_back(incoming, normed, spread, gain_vec):
    scaled = incoming * gain_vec
    back_grad = spread * (scaled - mean_of(scaled) - normed * mean_of(scaled * normed))
    return (back_grad, jnp.sum(incoming * normed, axis=1), jnp.sum(incoming, axis=1))


def layer(
    layer_input,
    segment_ids,
    qkv_weight,
    qkv_bias,
    out_weight,
    out_bias,
    norm1_gain,
    norm1_bias,
    up_weight,
    up_bias,
    down_weight,
    down_bias,
    norm2_gain,
    norm2_bias,
    output_grad,
):
    rows, width = layer_input.shape
    tensor_index = lax.axis_index("tensor")
    tensors = lax.axis_size("tensor")
    shards = lax.axis_size("shard")
    pairs = width // PAIR
    sharers = max(1, LEN // rows)
    seqs_here = max(1, rows // LEN)
    query_rows = min(rows, LEN)
    sharing = [list(range(i, i + sharers)) for i in range(0, tensors, sharers)]

    w_attn = gather_blocks(jnp.concatenate([qkv_weight, out_weight.T[None]]))
    w_up = gather_blocks(up_weight)
    w_down = gather_blocks(down_weight)
    w_attn = pair_blocks(w_attn)
    w_qkv, w_out = w_attn[:, :, :3], w_attn[:, :, 3]
    biases = lax.all_gather(
        jnp.concatenate([qkv_bias[0], qkv_bias[1], up_bias]), "tensor", axis=0, tiled=False
    )
    width_here, hidden_here = qkv_bias.shape[1], up_bias.shape[0]
    bias_q = biases[:, :width_here].reshape(pairs, 1, PAIR)
    bias_v = biases[:, width_here : 2 * width_here].reshape(pairs, 1, PAIR)
    bias_up = biases[:, 2 * width_here :].reshape(tensors, 1, hidden_here)

    def vec(values):
        return values.reshape(shards, 1, width // shards)

    def halves(rows_array):
        return rows_array.reshape(rows, shards, width // shards).transpose(1, 0, 2)

    def whole(blocks):
        return blocks.transpose(1, 0, 2).reshape(rows, width)

    first_seq = tensor_index * rows // LEN
    key_segments = lax.dynamic_slice_in_dim(segment_ids, first_seq, seqs_here, 0)
    query_start = tensor_index * rows % LEN
    query_segments = lax.dynamic_slice_in_dim(key_segments, query_start, query_rows, 1)
    bounds = block_bounds(query_segments, key_segments)
    q_mark, k_mark = doc_marks(query_segments, True), doc_marks(key_segments, False)

    def whole_rows(rows_array):
        if sharers == 1:
            return rows_array
        return lax.all_gather(rows_array, "tensor", axis_index_groups=sharing, axis=1, tiled=True)

    def own_rows(rows_array):
        if sharers == 1:
            return rows_array
        return lax.psum_scatter(
            rows_array, "tensor", axis_index_groups=sharing, scatter_dimension=1, tiled=True
        )

    tokens = halves(layer_input)
    projected = dot("std,snjdc->jntc", tokens, w_qkv)
    queries = ((projected[0] + bias_q).astype(jnp.bfloat16) * SCALE).astype(jnp.bfloat16)
    key_rows = whole_rows(projected[1].astype(jnp.bfloat16))
    value_rows = whole_rows((projected[2] + bias_v).astype(jnp.bfloat16))
    mixed, log_total = attend(queries, key_rows, value_rows, q_mark, k_mark, bounds)
    residual_one = tokens.astype(jnp.float32) + dot("ntc,sndc->std", mixed, w_out) + vec(out_bias)
    hidden_one, normed_one, spread_one = normalize(residual_one, vec(norm1_gain), vec(norm1_bias))
    hidden_low = hidden_one.astype(jnp.bfloat16)
    pre_act = dot("std,sndf->ntf", hidden_low, w_up) + bias_up
    normal_cdf = 0.5 * (1.0 + lax.erf(pre_act * (1.0 / math.sqrt(2.0))))
    normal_pdf = jnp.exp(-0.5 * pre_act * pre_act) * (1.0 / math.sqrt(2.0 * math.pi))
    activ = (pre_act * normal_cdf).astype(jnp.bfloat16)
    slope = (normal_cdf + pre_act * normal_pdf).astype(jnp.bfloat16)
    activ, slope = lax.optimization_barrier((activ, slope))
    residual_two = hidden_one + dot("ntf,snfd->std", activ, w_down) + vec(down_bias)
    final_out, normed_two, spread_two = normalize(residual_two, vec(norm2_gain), vec(norm2_bias))
    resid_two_grad, gain_two_grad, shift_two_grad = norm_back(
        halves(output_grad).astype(jnp.float32), normed_two, spread_two, vec(norm2_gain)
    )
    down_bias_part = jnp.sum(resid_two_grad, axis=1)
    branch_grad = resid_two_grad.astype(jnp.bfloat16)
    activ_grad = dot("std,snfd->ntf", branch_grad, w_down)
    pre_grad = activ_grad * slope.astype(jnp.float32)
    up_bias_part = jnp.sum(pre_grad, axis=1)
    pre_low = pre_grad.astype(jnp.bfloat16)
    ffn_grad = feed_forward_grads(branch_grad, activ, hidden_low, pre_low)
    ffn_owned = scatter_blocks(ffn_grad, (2,) + up_weight.shape)
    back_middle = dot("ntf,sndf->std", pre_low, w_up)
    resid_one_grad, gain_one_grad, shift_one_grad = norm_back(
        resid_two_grad + back_middle, normed_one, spread_one, vec(norm1_gain)
    )
    out_bias_part = jnp.sum(resid_one_grad, axis=1)
    attn_grad = resid_one_grad.astype(jnp.bfloat16)
    out_grad = dot("ntc,std->sncd", mixed, attn_grad).astype(jnp.bfloat16)
    mixed_grad = dot("std,sndc->ntc", attn_grad, w_out).astype(jnp.bfloat16)
    grad_type = jnp.bfloat16 if sharers == 1 else jnp.float32
    query_grad, key_grad, value_grad = attend_back(
        queries, key_rows, value_rows, q_mark, k_mark, bounds, log_total, mixed, mixed_grad, grad_type
    )
    key_grad, value_grad = own_rows(key_grad), own_rows(value_grad)
    proj_low = jnp.stack([query_grad, key_grad, value_grad]).astype(jnp.bfloat16)
    qkv_grad = [dot("ntc,std->sncd", proj_low[j], tokens).astype(jnp.bfloat16) for j in range(3)]
    attn_weight_grad = jnp.stack(qkv_grad + [out_grad], axis=2)
    attn_owned = scatter_blocks(
        unpair_blocks(attn_weight_grad, tensors), (4,) + out_weight.shape
    )
    back_input = dot("jntc,snjdc->std", proj_low, w_qkv)
    input_grad = resid_one_grad + back_input
    down_owned, up_owned = over_replicas(ffn_owned)
    down_owned = down_owned.T
    attn_owned = over_replicas(attn_owned)
    qkv_owned, out_owned = attn_owned[:3].transpose(0, 2, 1), attn_owned[3]
    parts = (
        jnp.sum(query_grad.astype(jnp.float32), axis=1),
        jnp.sum(value_grad.astype(jnp.float32), axis=1),
        up_bias_part,
        out_bias_part,
        gain_one_grad,
        shift_one_grad,
        down_bias_part,
        gain_two_grad,
        shift_two_grad,
    )
    parts = [part.reshape(-1) for part in parts]
    summed = jnp.concatenate(parts).reshape(-1, PAIR)
    for axis in EVERYONE:
        summed = sum_over(summed, axis)
    summed = summed.reshape(-1)
    ends = [0]
    for part in parts:
        ends.append(ends[-1] + part.shape[0])
    summed = [summed[ends[i] : ends[i + 1]] for i in range(len(parts))]
    qkv_bias_grad = lax.dynamic_slice_in_dim(
        jnp.stack(summed[:2]), tensor_index * width_here, width_here, 1
    )
    up_bias_grad = lax.dynamic_slice_in_dim(summed[2], tensor_index * hidden_here, hidden_here, 0)
    return (
        whole(final_out.astype(jnp.bfloat16)),
        whole(input_grad),
        qkv_owned,
        qkv_bias_grad,
        out_owned,
        summed[3],
        summed[4],
        summed[5],
        up_owned,
        up_bias_grad,
        down_owned,
        summed[6],
        summed[7],
        summed[8],
    )


def solution(mesh):
    placed = (
        P(("replica", "shard", "tensor"), None),
        P(("replica", "shard"), None),
        P(None, "shard", "tensor"),
        P(None, "tensor"),
        P("tensor", "shard"),
        P(),
        P(),
        P(),
        P("shard", "tensor"),
        P("tensor"),
        P("tensor", "shard"),
        P(),
        P(),
        P(),
        P(("replica", "shard", "tensor"), None),
    )
    return jax.shard_map(
        layer,
        mesh=mesh,
        in_specs=placed,
        out_specs=(
            P(("replica", "shard", "tensor"), None),
            P(("replica", "shard", "tensor"), None),
            P(None, "shard", "tensor"),
            P(None, "tensor"),
            P("tensor", "shard"),
            P(),
            P(),
            P(),
            P("shard", "tensor"),
            P("tensor"),
            P("tensor", "shard"),
            P(),
            P(),
            P(),
        ),
        check_vma=False,
    )
```
